128 devices in a mesh: seq: 16 (over y, x), head: 2 (over core), dp: 4 (over z).
Axes of the slice: x: 4, y: 4, z: 4, core: 2. Of those that a mesh axis runs over, the one named last changes fastest.
Arguments:
- queries: bfloat16 [8192, 2048], P(('dp', 'seq', 'head')), parts along dimension 0, may hold values from -48 to 48
- keys: bfloat16 [8192, 2048], P(('dp', 'seq', 'head')), parts along dimension 0, may hold values from -4 to 4
- writes: bfloat16 [8192, 2048], P(('dp', 'seq', 'head')), parts along dimension 0, may hold values from -48 to 48
- values: bfloat16 [8192, 2048], P(('dp', 'seq', 'head')), parts along dimension 0, may hold values from -4 to 4
- starts: int32 [8192], P(('dp', 'seq')), parts along dimension 0, may hold values from 0 to 2047, as said below
Outputs:
- attended: bfloat16 [8192, 2048], P(('dp', 'seq', 'head')), parts along dimension 0
The draws below stay inside these ranges and needn't reach their ends.
There are 4 independent parts, one for each index of `dp`. The reference program is written for one: setup_inputs(seed, part) draws one part's arguments, and reference() takes and returns one part's arrays. A program takes and returns all parts, laid end to end along the dimension named above; each array names one. Nothing has to cross between parts.
Inputs may be any that keep to these rules, and one draw needn't show every extreme that they name: starts[i] is the first position of position i's document: it never falls, is at most i, and equals i where a document begins.
All inputs are finite; a program needn't handle non-finite values.
Results may differ from the reference program's by a relative error of at most 0.004.
Values may be sent and summed in bfloat16 or wider, within the bound.
A program may use at most 64 MiB of HBM per device.

```python
import math
from functools import partial
import jax
import jax.numpy as jnp
from jax import lax

HD = 128
ROWS = 128
D = 2048
LEN = 2048
N_SEQ = 16


def draw_fields(key):
    base = jax.random.fold_in(key, 101)
    signs = jnp.where(jax.random.bernoulli(jax.random.fold_in(base, 5), 0.5, (D,)), 1.0, -1.0)
    positions = lax.iota(jnp.float32, LEN)
    ramp = positions / (4.5 * ROWS * math.sqrt(HD))
    key_level = jax.random.uniform(jax.random.fold_in(base, 6), (D,), jnp.float32, 1.5, 2.3)
    write_level = jax.random.uniform(jax.random.fold_in(base, 7), (D,), jnp.float32, 1.0, 2.0)
    key_noise = 0.5 * jnp.clip(jax.random.normal(jax.random.fold_in(base, 1), (LEN, D), jnp.float32), -4.0, 4.0)
    query_noise = 8.0 * jnp.clip(jax.random.normal(jax.random.fold_in(base, 2), (LEN, D), jnp.float32), -4.0, 4.0)
    write_noise = 3.0 * jnp.clip(jax.random.normal(jax.random.fold_in(base, 3), (LEN, D), jnp.float32), -4.0, 4.0)
    key_field = jnp.clip(signs[None, :] * (key_level[None, :] + ramp[:, None]) + key_noise, -4.0, 4.0)
    write_field = signs[None, :] * write_level[None, :] + write_noise
    query_field = query_noise
    query_field = jnp.clip(query_field, -48.0, 48.0)
    write_field = jnp.clip(write_field, -48.0, 48.0)
    key_field = jnp.clip(key_field, -4.0, 4.0)
    return (query_field, key_field, write_field)


def draw_queries(key, part):
    return draw_fields(key)[0].astype(jnp.bfloat16)


def draw_keys(key, part):
    return draw_fields(key)[1].astype(jnp.bfloat16)


def draw_writes(key, part):
    return draw_fields(key)[2].astype(jnp.bfloat16)


def draw_values(key, part):
    base = jax.random.fold_in(key, 303)
    signs = jnp.where(jax.random.bernoulli(jax.random.fold_in(base, 1), 0.5, (D,)), 1.0, -1.0)
    level = jax.random.uniform(jax.random.fold_in(base, 2), (D,), jnp.float32, 1.0, 2.0)
    noise = 0.5 * jnp.clip(jax.random.normal(jax.random.fold_in(base, 3), (LEN, D), jnp.float32), -3.0, 3.0)
    field = jnp.clip(signs[None, :] * level[None, :] + noise, -4.0, 4.0)
    return field.astype(jnp.bfloat16)


def draw_starts(key, part):
    base = jax.random.fold_in(key, 202)
    first_cut = jax.random.randint(jax.random.fold_in(base, 1), (), 13 * LEN // 16 + 1, 15 * LEN // 16)
    second_cut = jax.random.randint(jax.random.fold_in(base, 2), (), 15 * LEN // 16, LEN)
    positions = lax.iota(jnp.int32, LEN)
    return jnp.where(positions >= second_cut, second_cut, jnp.where(positions >= first_cut, first_cut, 0)).astype(jnp.int32)


def setup_inputs(seed: int = 0, part: int = 0) -> dict:
    arg_keys = jax.random.split(jax.random.key(seed), 6)
    part_splits = jax.random.split(jax.random.fold_in(arg_keys[5], part), 6)
    queries = draw_queries(jax.random.fold_in(jax.random.fold_in(arg_keys[5], part), 71), part)
    keys = draw_keys(jax.random.fold_in(jax.random.fold_in(arg_keys[5], part), 71), part)
    writes = draw_writes(jax.random.fold_in(jax.random.fold_in(arg_keys[5], part), 71), part)
    values = draw_values(jax.random.fold_in(jax.random.fold_in(arg_keys[5], part), 71), part)
    starts = draw_starts(jax.random.fold_in(jax.random.fold_in(arg_keys[5], part), 71), part)
    return {"queries": queries, "keys": keys, "writes": writes, "values": values, "starts": starts}


masked_score = -1e+30

def attend_head(packed, starts):
    query_head, key_head, write_head, value_head = packed
    positions = jnp.arange(LEN, dtype=jnp.int32)
    after_start = positions[None, :] >= starts[:, None]
    strict_mask = (positions[None, :] < positions[:, None]) & after_start
    causal_mask = (positions[None, :] <= positions[:, None]) & after_start
    key_float = key_head.astype(jnp.float32)
    score_write = jnp.dot(write_head.astype(jnp.float32), key_float.T, precision=lax.Precision.HIGHEST) * HD ** (-0.5)
    score_query = jnp.dot(query_head.astype(jnp.float32), key_float.T, precision=lax.Precision.HIGHEST) * HD ** (-0.5)
    peak_write = jnp.maximum(0.0, jnp.max(jnp.where(strict_mask, score_write, masked_score), axis=1))
    write_weights = jnp.exp(jnp.where(strict_mask, score_write - peak_write[:, None], masked_score))
    total_write = jnp.exp(-peak_write) + jnp.sum(write_weights, axis=1)
    peak_query = jnp.max(jnp.where(causal_mask, score_query, masked_score), axis=1)
    query_weights = jnp.exp(jnp.where(causal_mask, score_query - peak_query[:, None], masked_score))
    total_query = jnp.sum(query_weights, axis=1)
    write_low = write_weights.astype(jnp.bfloat16)
    solved_all = jnp.zeros((LEN, HD), jnp.bfloat16)
    for shard in range(N_SEQ):
        lower = shard * ROWS
        upper = lower + ROWS
        numerator = jnp.dot(write_low[lower:upper].astype(jnp.float32), solved_all.astype(jnp.float32), preferred_element_type=jnp.float32)
        right_side = value_head[lower:upper].astype(jnp.float32) - numerator / total_write[lower:upper, None]
        diagonal = write_weights[lower:upper, lower:upper] / total_write[lower:upper, None]
        solved_part = jax.scipy.linalg.solve_triangular(diagonal, right_side, lower=True, unit_diagonal=True)
        solved_all = solved_all.at[lower:upper].set(solved_part.astype(jnp.bfloat16))
    readout = jnp.dot(query_weights.astype(jnp.bfloat16).astype(jnp.float32), solved_all.astype(jnp.float32), preferred_element_type=jnp.float32)
    return (readout / total_query[:, None]).astype(jnp.bfloat16)

def by_heads(array):
    head_count = D // HD
    return jnp.transpose(array.reshape(LEN, head_count, HD), (1, 0, 2))

def reference(queries, keys, writes, values, starts):
    packed = (by_heads(queries), by_heads(keys), by_heads(writes), by_heads(values))
    outputs = lax.map(partial(attend_head, starts=starts), packed)
    return jnp.transpose(outputs, (1, 0, 2)).reshape(LEN, D)
```

```python
import functools
import math

import jax
import jax.numpy as jnp
from jax import lax
from jax.experimental import pallas as pl
from jax.experimental.pallas import tpu as pltpu
from jax.sharding import PartitionSpec as P

HD = 128
BLK = 128
HALF = 64
MASKED = -1e30
SCALE2 = HD ** (-0.5) * math.log2(math.e)
MESH = pl.DeviceIdType.MESH
F32 = jnp.float32
BF16 = jnp.bfloat16
NT = (((1,), (1,)), ((), ()))


def dot(a, b):
    return jnp.dot(a, b, preferred_element_type=F32)


def kernel(n, group, q_ref, k_ref, w_ref, v_ref, st_ref, out_ref, abuf, kbuf, vbuf, sbuf, ebuf, sscr,
           lbuf, xbuf, ubuf, uland, obuf, dbuf, send_sem, own_sem, st_send, recv_sem, st_recv, ku_send, u_recv,
           o_send, o_recv):
    me = lax.axis_index("seq")
    core = lax.axis_index("head")
    length = n * BLK

    def chip(step):
        return lax.rem(me + step, n)

    barrier = pltpu.get_barrier_semaphore()

    def greet(step, carry):
        for c in (0, 1):
            pl.semaphore_signal(barrier, inc=1, device_id={"seq": chip(step), "head": c}, device_id_type=MESH)
        return carry

    lax.fori_loop(1, n, greet, 0)
    pl.semaphore_signal(barrier, inc=1, device_id={"head": 1 - core}, device_id_type=MESH)
    pl.semaphore_wait(barrier, 2 * n - 1)

    my_rows = pl.ds(pl.multiple_of(me * BLK + core * HALF, HALF), HALF)
    streams = ((k_ref, kbuf, 0), (w_ref, abuf, 0), (v_ref, vbuf, 0), (q_ref, abuf, 1))

    def strip(ref, head):
        return ref.at[:, pl.ds(pl.multiple_of(head * HD, HD), HD)]

    def remote(stream, step):
        src, dst, c = streams[stream]
        target = chip(step)
        return pltpu.make_async_remote_copy(
            src_ref=strip(src, target), dst_ref=dst.at[my_rows], send_sem=send_sem.at[stream, step],
            recv_sem=recv_sem.at[stream], device_id={"seq": target, "head": c}, device_id_type=MESH)

    def starts_copy(step, c):
        return pltpu.make_async_remote_copy(
            src_ref=st_ref, dst_ref=sbuf.at[me], send_sem=st_send.at[step, c], recv_sem=st_recv,
            device_id={"seq": chip(step), "head": c}, device_id_type=MESH)

    for stream in range(4):
        src, dst, c = streams[stream]

        @pl.when(core == c)
        def _():
            pltpu.make_async_copy(strip(src, me), dst.at[my_rows], recv_sem.at[stream]).start()

        @pl.when(core != c)
        def _():
            remote(stream, 0).start()

        def send(step, carry):
            remote(stream, step).start()
            return carry

        lax.fori_loop(1, n, send, 0)
        if stream == 0:
            pltpu.make_async_copy(st_ref, sbuf.at[me], st_recv).start()
            for c in (0, 1):
                @pl.when(core == c)
                def _():
                    def send_starts(step, carry):
                        starts_copy(step, c).start()
                        return carry

                    lax.fori_loop(1, n, send_starts, 0)

    def wait_all(buf, sem):
        pltpu.make_async_copy(buf, buf, sem).wait()

    def keys_over():
        return pltpu.make_async_remote_copy(
            src_ref=kbuf, dst_ref=kbuf, send_sem=ku_send.at[n], recv_sem=recv_sem.at[4],
            device_id={"head": 1}, device_id_type=MESH)

    def solved_over(b):
        return pltpu.make_async_remote_copy(
            src_ref=ubuf.at[pl.ds(pl.multiple_of(b * BLK, BLK), BLK)], dst_ref=uland.at[b], send_sem=ku_send.at[b],
            recv_sem=u_recv.at[b], device_id={"head": 1}, device_id_type=MESH)

    def block_rows(b):
        return pl.ds(pl.multiple_of(b * BLK, BLK), BLK)

    def weights(solve):
        for g in range(n // group):
            def one(i, carry):
                b = g * group + i
                rows = abuf[block_rows(b), :]
                first = jnp.broadcast_to(sbuf[b].astype(F32), (BLK, BLK)).T.astype(jnp.int32)
                lane = lax.broadcasted_iota(jnp.int32, (BLK, BLK), 1)
                row = lax.broadcasted_iota(jnp.int32, (BLK, BLK), 0) + b * BLK
                top = jnp.full((BLK, BLK), 0.0 if solve else MASKED, F32)
                for j in range((g + 1) * group):
                    score = lax.dot_general(rows, kbuf[j * BLK:(j + 1) * BLK, :], NT, preferred_element_type=F32)
                    col = lane + j * BLK
                    allowed = col >= first
                    if j >= g * group:
                        allowed = allowed & ((col < row) if solve else (col <= row))
                    score = jnp.where(allowed, score, MASKED)
                    top = jnp.maximum(top, score)
                    sscr[:, j * BLK:(j + 1) * BLK] = score
                peak = jnp.max(top, axis=1, keepdims=True)
                total = jnp.zeros((BLK, BLK), F32)
                for j in range((g + 1) * group):
                    e = jnp.exp2((sscr[:, j * BLK:(j + 1) * BLK] - peak) * SCALE2)
                    total = total + e
                    ebuf[b, :, j * BLK:(j + 1) * BLK] = e.astype(BF16)
                    if solve and j >= g * group:
                        sscr[:, j * BLK:(j + 1) * BLK] = e
                den = jnp.sum(total, axis=1, keepdims=True)
                if solve:
                    den = den + jnp.exp2(-peak * SCALE2)
                inv = 1.0 / den
                dbuf[b] = jnp.broadcast_to(inv, (BLK, BLK))
                if solve:
                    lbuf[b] = sscr[:, block_rows(b)] * inv
                return carry

            lax.fori_loop(0, group, one, 0)

    def invert(b):
        low = lbuf[b]
        eye = (lax.broadcasted_iota(jnp.int32, (BLK, BLK), 0)
               == lax.broadcasted_iota(jnp.int32, (BLK, BLK), 1)).astype(F32)
        low_hi = low.astype(BF16)
        low_lo = (low - low_hi.astype(F32)).astype(BF16)
        total = eye - low
        power = dot(low_hi, low_hi).astype(BF16)
        for step in range(1, 7):
            if step < 6:
                both = dot(jnp.concatenate([total.astype(BF16), power], axis=0), power)
                total = total + both[:BLK]
                power = both[BLK:].astype(BF16)
            else:
                total = total + dot(total.astype(BF16), power)
        guess = total.astype(BF16)
        guess_wide = guess.astype(F32)
        residual = eye - guess_wide - dot(jnp.concatenate([low_hi, low_lo], axis=1),
                                          jnp.concatenate([guess, guess], axis=0))
        better = guess_wide + dot(guess, residual.astype(BF16))
        hi = better.astype(BF16)
        lo = (better - hi.astype(F32)).astype(BF16)
        xbuf[b] = jnp.concatenate([hi, lo, hi], axis=1)

    @pl.when(core == 0)
    def _():
        ubuf[...] = jnp.zeros_like(ubuf)
        wait_all(kbuf, recv_sem.at[0])
        keys_over().start()
        wait_all(sbuf, st_recv)
        wait_all(abuf, recv_sem.at[1])
        weights(True)

        def invert_some(i, carry):
            for j in range(4):
                invert(i * 4 + j)
            return carry

        lax.fori_loop(0, n // 4, invert_some, 0)
        wait_all(vbuf, recv_sem.at[2])
        for g in range(n // group):
            def one(i, carry):
                b = g * group + i
                width = (g + 1) * group * BLK
                numerator = dot(ebuf[b, :, 0:width], ubuf[0:width, :])
                rhs = vbuf[block_rows(b), :].astype(F32) - numerator * dbuf[b]
                hi = rhs.astype(BF16)
                lo = (rhs - hi.astype(F32)).astype(BF16)
                ubuf[block_rows(b), :] = dot(xbuf[b], jnp.concatenate([hi, hi, lo], axis=0)).astype(BF16)
                solved_over(b).start()
                return carry

            lax.fori_loop(0, group, one, 0)

    def readout_copy(b, half):
        return pltpu.make_async_remote_copy(
            src_ref=obuf.at[b, pl.ds(half * HALF, HALF)], dst_ref=strip(out_ref, me), send_sem=o_send.at[b, half],
            recv_sem=o_recv, device_id={"seq": b, "head": half}, device_id_type=MESH)

    @pl.when(core == 1)
    def _():
        ubuf[...] = jnp.zeros_like(ubuf)
        wait_all(sbuf, st_recv)
        wait_all(abuf, recv_sem.at[3])
        wait_all(kbuf, recv_sem.at[4])
        weights(False)
        for g in range(n // group):
            def one(i, carry):
                b = g * group + i
                width = (g + 1) * group * BLK
                wait_all(uland.at[b], u_recv.at[b])
                ubuf[block_rows(b), :] = uland[b]
                numerator = dot(ebuf[b, :, 0:width], ubuf[0:width, :])
                obuf[b] = (numerator * dbuf[b]).astype(BF16)
                readout_copy(b, 0).start()

                @pl.when(b != me)
                def _():
                    readout_copy(b, 1).start()

                @pl.when(b == me)
                def _():
                    pltpu.make_async_copy(obuf.at[b, pl.ds(HALF, HALF)], strip(out_ref, me), o_recv).start()

                return carry

            lax.fori_loop(0, group, one, 0)

    wait_all(out_ref, o_recv)

    for stream in range(4):
        @pl.when(core != streams[stream][2])
        def _():
            remote(stream, 0).wait_send()

        def sent(step, carry):
            remote(stream, step).wait_send()
            return carry

        lax.fori_loop(1, n, sent, 0)
    for c in (0, 1):
        @pl.when(core == c)
        def _():
            def starts_sent(step, carry):
                starts_copy(step, c).wait_send()
                return carry

            lax.fori_loop(1, n, starts_sent, 0)

    @pl.when(core == 0)
    def _():
        keys_over().wait_send()

        def solved_sent(b, carry):
            solved_over(b).wait_send()
            return carry

        lax.fori_loop(0, n, solved_sent, 0)

    @pl.when(core == 1)
    def _():
        def readout_sent(b, carry):
            readout_copy(b, 0).wait_send()

            @pl.when(b != me)
            def _():
                readout_copy(b, 1).wait_send()

            return carry

        lax.fori_loop(0, n, readout_sent, 0)


def solution(mesh):
    n = mesh.shape["seq"]
    group = 4

    def step(queries, keys, writes, values, starts):
        features = queries.shape[1]
        length = n * BLK
        hbm = pl.BlockSpec(memory_space=pl.ANY)
        dma = pltpu.SemaphoreType.DMA
        return pl.pallas_call(
            functools.partial(kernel, n, group),
            out_shape=jax.ShapeDtypeStruct((HALF, features), BF16),
            in_specs=[hbm] * 5,
            out_specs=hbm,
            scratch_shapes=[
                pltpu.VMEM((length, HD), BF16),
                pltpu.VMEM((length, HD), BF16),
                pltpu.VMEM((length, HD), BF16),
                pltpu.VMEM((n, 1, BLK), jnp.int32),
                pltpu.VMEM((n, BLK, length), BF16),
                pltpu.VMEM((BLK, length), F32),
                pltpu.VMEM((n, BLK, BLK), F32),
                pltpu.VMEM((n, BLK, 3 * BLK), BF16),
                pltpu.VMEM((length, HD), BF16),
                pltpu.VMEM((n, BLK, HD), BF16),
                pltpu.VMEM((n, BLK, HD), BF16),
                pltpu.VMEM((n, BLK, BLK), F32),
                dma((4, n)),
                dma,
                dma((n, 2)),
                dma((5,)),
                dma,
                dma((n + 1,)),
                dma((n,)),
                dma((n, 2)),
                dma,
            ],
            compiler_params=pltpu.CompilerParams(collective_id=0, has_side_effects=True,
                                                 vmem_limit_bytes=48 * 1024 * 1024),
        )(queries, keys, writes, values, starts.reshape(1, BLK))

    rows = P(("dp", "seq", "head"), None)
    return jax.shard_map(step, mesh=mesh, in_specs=(rows, rows, rows, rows, P(("dp", "seq"))), out_specs=rows,
                         check_vma=False)
```

```python
import functools
import math

import jax
import jax.numpy as jnp
from jax import lax
from jax.experimental import pallas as pl
from jax.experimental.pallas import tpu as pltpu
from jax.sharding import PartitionSpec as P

HD = 128
BLK = 128
HALF = 64
MASKED = -1e30
SCALE2 = HD ** (-0.5) * math.log2(math.e)
MESH = pl.DeviceIdType.MESH
F32 = jnp.float32
BF16 = jnp.bfloat16
NT = (((1,), (1,)), ((), ()))


def dot(a, b):
    return jnp.dot(a, b, preferred_element_type=F32)


def kernel(n, q_ref, k_ref, w_ref, v_ref, st_ref, out_ref, abuf, kbuf, vbuf, sbuf, ebuf, sscr, mbuf, ybuf, ubuf,
           obuf, dbuf, send_sem, st_send, recv_sem, st_recv, ku_send, u_recv, o_send, o_recv):
    me = lax.axis_index("seq")
    core = lax.axis_index("head")

    def chip(step):
        return lax.rem(me + step, n)

    barrier = pltpu.get_barrier_semaphore()

    def greet(step, carry):
        for c in (0, 1):
            pl.semaphore_signal(barrier, inc=1, device_id={"seq": chip(step), "head": c}, device_id_type=MESH)
        return carry

    lax.fori_loop(1, n, greet, 0)
    pl.semaphore_signal(barrier, inc=1, device_id={"head": 1 - core}, device_id_type=MESH)
    pl.semaphore_wait(barrier, 2 * n - 1)

    my_rows = pl.ds(pl.multiple_of(me * BLK + core * HALF, HALF), HALF)
    streams = ((k_ref, kbuf, 0), (w_ref, abuf, 0), (v_ref, vbuf, 0), (q_ref, abuf, 1))

    def strip(ref, head):
        return ref.at[:, pl.ds(pl.multiple_of(head * HD, HD), HD)]

    def remote(stream, step):
        src, dst, c = streams[stream]
        target = chip(step)
        return pltpu.make_async_remote_copy(
            src_ref=strip(src, target), dst_ref=dst.at[my_rows], send_sem=send_sem.at[stream, step],
            recv_sem=recv_sem.at[stream], device_id={"seq": target, "head": c}, device_id_type=MESH)

    def starts_copy(step, c):
        return pltpu.make_async_remote_copy(
            src_ref=st_ref, dst_ref=sbuf.at[me], send_sem=st_send.at[step, c], recv_sem=st_recv,
            device_id={"seq": chip(step), "head": c}, device_id_type=MESH)

    for stream in range(4):
        src, dst, c = streams[stream]

        @pl.when(core == c)
        def _():
            pltpu.make_async_copy(strip(src, me), dst.at[my_rows], recv_sem.at[stream]).start()

        @pl.when(core != c)
        def _():
            remote(stream, 0).start()

        def send(step, carry):
            remote(stream, step).start()
            return carry

        lax.fori_loop(1, n, send, 0)
        if stream == 0:
            pltpu.make_async_copy(st_ref, sbuf.at[me], st_recv).start()
            for c in (0, 1):
                @pl.when(core == c)
                def _():
                    def send_starts(step, carry):
                        starts_copy(step, c).start()
                        return carry

                    lax.fori_loop(1, n, send_starts, 0)

    def wait_all(buf, sem):
        pltpu.make_async_copy(buf, buf, sem).wait()

    def keys_over():
        return pltpu.make_async_remote_copy(
            src_ref=kbuf, dst_ref=kbuf, send_sem=ku_send.at[n], recv_sem=recv_sem.at[4],
            device_id={"head": 1}, device_id_type=MESH)

    def solved_over(p):
        return pltpu.make_async_remote_copy(
            src_ref=ubuf.at[p], dst_ref=ubuf.at[p], send_sem=ku_send.at[p], recv_sem=u_recv.at[p],
            device_id={"head": 1}, device_id_type=MESH)

    pairs = n // 2
    wide = 2 * BLK

    def weights(p, solve):
        rows = abuf[p * wide:(p + 1) * wide, :]
        sub = lax.broadcasted_iota(jnp.int32, (8, wide), 0)
        first = jnp.concatenate([sbuf[2 * p], sbuf[2 * p + 1]], axis=1) - sub
        limit = lax.broadcasted_iota(jnp.int32, (8, wide), 1) + p * wide - sub
        top = jnp.full((8, wide), 0.0 if solve else MASKED, F32)
        tiles = 2 * p + 2
        for j in range(tiles):
            score = lax.dot_general(kbuf[j * BLK:(j + 1) * BLK, :], rows, NT, preferred_element_type=F32)
            score = score.reshape(BLK // 8, 8, wide)
            key = lax.broadcasted_iota(jnp.int32, score.shape, 0) * 8 + j * BLK
            allowed = key >= first
            if j >= 2 * p:
                allowed = allowed & ((key < limit) if solve else (key <= limit))
            score = jnp.where(allowed, score, MASKED)
            top = jnp.maximum(top, jnp.max(score, axis=0))
            sscr[j * BLK:(j + 1) * BLK, :] = score.reshape(BLK, wide)
        peak = jnp.max(top, axis=0, keepdims=True)
        total = jnp.zeros((8, wide), F32)
        for j in range(tiles):
            e = jnp.exp2((sscr[j * BLK:(j + 1) * BLK, :] - peak) * SCALE2)
            total = total + jnp.sum(e.reshape(BLK // 8, 8, wide), axis=0)
            ebuf[p, j * BLK:(j + 1) * BLK, :] = e.astype(BF16)
            if solve and j >= 2 * p:
                mbuf[p, (j - 2 * p) * BLK:(j - 2 * p + 1) * BLK, :] = e
        den = jnp.sum(total, axis=0, keepdims=True)
        if solve:
            den = den + jnp.exp2(-peak * SCALE2)
        dbuf[p] = 1.0 / den
        if solve:
            mbuf[p] = mbuf[p] * dbuf[p]

    def diagonal(x):
        zero = jnp.zeros((BLK, BLK), BF16)
        return jnp.concatenate([jnp.concatenate([x[:, :BLK], zero], axis=1),
                                jnp.concatenate([zero, x[:, BLK:]], axis=1)], axis=0)

    def split(x):
        hi = x.astype(BF16)
        return hi, (x - hi.astype(F32)).astype(BF16)

    def product(a, b):
        (a_hi, a_lo), (b_hi, b_lo) = split(a), split(b)
        return dot(jnp.concatenate([a_hi, a_lo, a_hi], axis=1), jnp.concatenate([b_hi, b_hi, b_lo], axis=0))

    def invert(which):
        eye = (lax.broadcasted_iota(jnp.int32, (BLK, BLK), 0)
               == lax.broadcasted_iota(jnp.int32, (BLK, BLK), 1)).astype(F32)
        eye = jnp.concatenate([eye, eye], axis=1)
        upper = {p: jnp.concatenate([mbuf[p, :BLK, :BLK], mbuf[p, BLK:, BLK:]], axis=1) for p in which}
        parts = {p: split(upper[p]) for p in which}
        total = {p: eye - upper[p] for p in which}
        power = {p: dot(parts[p][0], diagonal(parts[p][0])).astype(BF16) for p in which}
        for step in range(1, 7):
            for p in which:
                if step < 6:
                    both = dot(jnp.concatenate([total[p].astype(BF16), power[p]], axis=0), diagonal(power[p]))
                    total[p] = total[p] + both[:BLK]
                    power[p] = both[BLK:].astype(BF16)
                else:
                    total[p] = total[p] + dot(total[p].astype(BF16), diagonal(power[p]))
        guess = {p: total[p].astype(BF16) for p in which}
        again = {p: dot(jnp.concatenate(parts[p], axis=0), diagonal(guess[p])) for p in which}
        better = {}
        for p in which:
            residual = eye - guess[p].astype(F32) - again[p][:BLK] - again[p][BLK:]
            better[p] = guess[p].astype(F32) + dot(guess[p], diagonal(residual.astype(BF16)))
        inner = {p: product(mbuf[p, :BLK, BLK:], better[p][:, BLK:]) for p in which}
        for p in which:
            corner = -product(better[p][:, :BLK], inner[p])
            whole = jnp.concatenate(
                [jnp.concatenate([better[p][:, :BLK], corner], axis=1),
                 jnp.concatenate([jnp.zeros((BLK, BLK), F32), better[p][:, BLK:]], axis=1)], axis=0)
            hi, lo = split(whole)
            ybuf[p, :wide] = hi
            ybuf[p, wide:2 * wide] = hi
            ybuf[p, 2 * wide:] = lo

    def solved(count):
        return jnp.concatenate([ubuf[q] for q in range(count)], axis=1)

    @pl.when(core == 0)
    def _():
        wait_all(kbuf, recv_sem.at[0])
        keys_over().start()
        wait_all(sbuf, st_recv)
        wait_all(abuf, recv_sem.at[1])
        for p in range(pairs):
            weights(p, True)
        for g in range(0, pairs, 4):
            invert(range(g, min(g + 4, pairs)))
        wait_all(vbuf, recv_sem.at[2])
        for p in range(pairs):
            rhs = vbuf[p * wide:(p + 1) * wide, :].astype(F32).T
            if p:
                rhs = rhs - dot(solved(p), ebuf[p, :p * wide, :]) * dbuf[p]
            hi, lo = split(rhs)
            ubuf[p] = dot(jnp.concatenate([hi, lo, hi], axis=1), ybuf[p]).astype(BF16)
            solved_over(p).start()

    def readout_copy(p, r, half):
        return pltpu.make_async_remote_copy(
            src_ref=obuf.at[p, pl.ds((2 * r + half) * HALF, HALF)], dst_ref=strip(out_ref, me),
            send_sem=o_send.at[2 * p + r, half], recv_sem=o_recv, device_id={"seq": 2 * p + r, "head": half},
            device_id_type=MESH)

    @pl.when(core == 1)
    def _():
        wait_all(sbuf, st_recv)
        wait_all(abuf, recv_sem.at[3])
        wait_all(kbuf, recv_sem.at[4])
        for p in range(pairs):
            weights(p, False)
        for p in range(pairs):
            if p:
                before = dot(solved(p), ebuf[p, :p * wide, :])
            wait_all(ubuf.at[p], u_recv.at[p])
            read = dot(ubuf[p], ebuf[p, p * wide:(p + 1) * wide, :])
            if p:
                read = read + before
            obuf[p] = (read * dbuf[p]).T.astype(BF16)
            for r in (0, 1):
                readout_copy(p, r, 0).start()

                @pl.when(me != 2 * p + r)
                def _():
                    readout_copy(p, r, 1).start()

                @pl.when(me == 2 * p + r)
                def _():
                    pltpu.make_async_copy(obuf.at[p, pl.ds((2 * r + 1) * HALF, HALF)], strip(out_ref, me),
                                          o_recv).start()

    wait_all(out_ref, o_recv)

    for stream in range(4):
        @pl.when(core != streams[stream][2])
        def _():
            remote(stream, 0).wait_send()

        def sent(step, carry):
            remote(stream, step).wait_send()
            return carry

        lax.fori_loop(1, n, sent, 0)
    for c in (0, 1):
        @pl.when(core == c)
        def _():
            def starts_sent(step, carry):
                starts_copy(step, c).wait_send()
                return carry

            lax.fori_loop(1, n, starts_sent, 0)

    @pl.when(core == 0)
    def _():
        keys_over().wait_send()

        def solved_sent(p, carry):
            solved_over(p).wait_send()
            return carry

        lax.fori_loop(0, pairs, solved_sent, 0)

    @pl.when(core == 1)
    def _():
        for p in range(pairs):
            for r in (0, 1):
                readout_copy(p, r, 0).wait_send()

                @pl.when(me != 2 * p + r)
                def _():
                    readout_copy(p, r, 1).wait_send()


def solution(mesh):
    n = mesh.shape["seq"]

    def step(queries, keys, writes, values, starts):
        features = queries.shape[1]
        length = n * BLK
        hbm = pl.BlockSpec(memory_space=pl.ANY)
        dma = pltpu.SemaphoreType.DMA
        return pl.pallas_call(
            functools.partial(kernel, n),
            out_shape=jax.ShapeDtypeStruct((HALF, features), BF16),
            in_specs=[hbm] * 5,
            out_specs=hbm,
            scratch_shapes=[
                pltpu.VMEM((length, HD), BF16),
                pltpu.VMEM((length, HD), BF16),
                pltpu.VMEM((length, HD), BF16),
                pltpu.VMEM((n, 1, BLK), jnp.int32),
                pltpu.VMEM((n // 2, length, 2 * BLK), BF16),
                pltpu.VMEM((length, 2 * BLK), F32),
                pltpu.VMEM((n // 2, 2 * BLK, 2 * BLK), F32),
                pltpu.VMEM((n // 2, 6 * BLK, 2 * BLK), BF16),
                pltpu.VMEM((n // 2, HD, 2 * BLK), BF16),
                pltpu.VMEM((n // 2, 2 * BLK, HD), BF16),
                pltpu.VMEM((n // 2, 1, 2 * BLK), F32),
                dma((4, n)),
                dma((n, 2)),
                dma((5,)),
                dma,
                dma((n + 1,)),
                dma((n // 2,)),
                dma((n, 2)),
                dma,
            ],
            compiler_params=pltpu.CompilerParams(collective_id=0, has_side_effects=True,
                                                 vmem_limit_bytes=67_043_328),
        )(queries, keys, writes, values, starts.reshape(1, BLK))

    rows = P(("dp", "seq", "head"), None)
    return jax.shard_map(step, mesh=mesh, in_specs=(rows, rows, rows, rows, P(("dp", "seq"))), out_specs=rows,
                         check_vma=False)
```

```python
import functools
import math

import jax
import jax.numpy as jnp
from jax import lax
from jax.experimental import pallas as pl
from jax.experimental.pallas import tpu as pltpu
from jax.sharding import PartitionSpec as P

HD = 128
BLK = 128
HALF = 64
MASKED = -1e30
SCALE2 = HD ** (-0.5) * math.log2(math.e)
MESH = pl.DeviceIdType.MESH
F32 = jnp.float32
BF16 = jnp.bfloat16
NT = (((1,), (1,)), ((), ()))


def dot(a, b):
    return jnp.dot(a, b, preferred_element_type=F32)


def kernel(n, q_ref, k_ref, w_ref, v_ref, st_ref, out_ref, qbuf, kbuf, wbuf, vbuf, sbuf, bias, ebuf, fbuf, sscr, mbuf,
           ybuf, ubuf, obuf, dbuf, fden, send_sem, st_send, recv_sem, k_send, k_recv, st_recv, u_send, u_recv, o_send,
           o_recv):
    me = lax.axis_index("seq")
    core = lax.axis_index("head")

    def chip(step):
        return lax.rem(me + step, n)

    barrier = pltpu.get_barrier_semaphore()

    def greet(step, carry):
        for c in (0, 1):
            pl.semaphore_signal(barrier, inc=1, device_id={"seq": chip(step), "head": c}, device_id_type=MESH)
        return carry

    lax.fori_loop(1, n, greet, 0)
    pl.semaphore_signal(barrier, inc=1, device_id={"head": 1 - core}, device_id_type=MESH)
    pl.semaphore_wait(barrier, 2 * n - 1)

    my_rows = pl.ds(pl.multiple_of(me * BLK + core * HALF, HALF), HALF)
    half_index = me // (n // 2)
    solver = 1 - half_index
    reader = jnp.where(me >= n - 2, 0, 1)
    streams = ((k_ref, kbuf, solver), (w_ref, wbuf, solver), (v_ref, vbuf, solver), (q_ref, qbuf, reader))

    def strip(ref, head):
        return ref.at[:, pl.ds(pl.multiple_of(head * HD, HD), HD)]

    def remote(stream, step):
        src, dst, c = streams[stream]
        target = chip(step)
        return pltpu.make_async_remote_copy(
            src_ref=strip(src, target), dst_ref=dst.at[my_rows], send_sem=send_sem.at[stream, step],
            recv_sem=recv_sem.at[stream, half_index], device_id={"seq": target, "head": c}, device_id_type=MESH)

    def starts_copy(step, c):
        return pltpu.make_async_remote_copy(
            src_ref=st_ref, dst_ref=sbuf.at[me], send_sem=st_send.at[step, c], recv_sem=st_recv,
            device_id={"seq": chip(step), "head": c}, device_id_type=MESH)

    pltpu.make_async_copy(st_ref, sbuf.at[me], st_recv).start()
    for c in (0, 1):
        @pl.when(core == c)
        def _():
            def send_starts(step, carry):
                starts_copy(step, c).start()
                return carry

            lax.fori_loop(1, n, send_starts, 0)

    def send_stream(stream):
        src, dst, c = streams[stream]

        @pl.when(core == c)
        def _():
            pltpu.make_async_copy(strip(src, me), dst.at[my_rows], recv_sem.at[stream, half_index]).start()

        @pl.when(core != c)
        def _():
            remote(stream, 0).start()

        def send(step, carry):
            remote(stream, step).start()
            return carry

        lax.fori_loop(1, n, send, 0)

    send_stream(0)
    send_stream(1)

    @pl.when(half_index == 0)
    def _():
        send_stream(2)
        send_stream(3)

    @pl.when(half_index != 0)
    def _():
        send_stream(3)
        send_stream(2)

    def wait_all(buf, sem):
        pltpu.make_async_copy(buf, buf, sem).wait()

    def wait_rows(buf, stream, first, last):
        if last > first:
            wait_all(buf.at[first * BLK:last * BLK], recv_sem.at[stream, first // (n // 2)])

    def keys_over():
        mine = kbuf.at[pl.ds(pl.multiple_of((1 - core) * (n * HALF), n * HALF), n * HALF)]
        return pltpu.make_async_remote_copy(src_ref=mine, dst_ref=mine, send_sem=k_send, recv_sem=k_recv,
                                            device_id={"head": 1 - core}, device_id_type=MESH)

    def solved_over(p):
        return pltpu.make_async_remote_copy(
            src_ref=ubuf.at[p], dst_ref=ubuf.at[p], send_sem=u_send.at[p], recv_sem=u_recv.at[p],
            device_id={"head": 1 - core}, device_id_type=MESH)

    pairs = n // 2
    wide = 2 * BLK

    half_pairs = pairs // 2

    def tile_of(p, j):
        return p * (p + 1) + j

    def mask(which):
        for p in which:
            first = jnp.concatenate([sbuf[2 * p], sbuf[2 * p + 1]], axis=1)
            first = first - lax.broadcasted_iota(jnp.int32, (8, wide), 0)
            for j in range(2 * p + 2):
                key = lax.broadcasted_iota(jnp.int32, (BLK // 8, 8, wide), 0) * 8 + j * BLK
                bias[tile_of(p, j)] = jnp.where(key >= first, 0.0, MASKED).reshape(BLK, wide)

    def weights(p, solve):
        rows = (wbuf if solve else qbuf)[p * wide:(p + 1) * wide, :]
        into, den_into = (ebuf, dbuf) if solve else (fbuf, fden)
        limit = (lax.broadcasted_iota(jnp.int32, (8, wide), 1) + p * wide
                 - lax.broadcasted_iota(jnp.int32, (8, wide), 0))
        top = jnp.full((8, wide), 0.0 if solve else MASKED, F32)
        tiles = 2 * p + 2
        for j in range(tiles):
            score = lax.dot_general(kbuf[j * BLK:(j + 1) * BLK, :], rows, NT, preferred_element_type=F32)
            score = (score + bias[tile_of(p, j)]).reshape(BLK // 8, 8, wide)
            if j >= 2 * p:
                key = lax.broadcasted_iota(jnp.int32, score.shape, 0) * 8 + j * BLK
                score = jnp.where((key < limit) if solve else (key <= limit), score, MASKED)
            top = jnp.maximum(top, jnp.max(score, axis=0))
            sscr[j * BLK:(j + 1) * BLK, :] = score.reshape(BLK, wide)
        peak = jnp.max(top, axis=0, keepdims=True)
        total = jnp.zeros((8, wide), F32)
        for j in range(tiles):
            e = jnp.exp2((sscr[j * BLK:(j + 1) * BLK, :] - peak) * SCALE2)
            total = total + jnp.sum(e.reshape(BLK // 8, 8, wide), axis=0)
            into[p, j * BLK:(j + 1) * BLK, :] = e.astype(BF16)
            if solve and j >= 2 * p:
                mbuf[p, (j - 2 * p) * BLK:(j - 2 * p + 1) * BLK, :] = e
        den = jnp.sum(total, axis=0, keepdims=True)
        if solve:
            den = den + jnp.exp2(-peak * SCALE2)
        den_into[p] = 1.0 / den
        if solve:
            mbuf[p] = mbuf[p] * den_into[p]

    def diagonal(x):
        zero = jnp.zeros((BLK, BLK), BF16)
        return jnp.concatenate([jnp.concatenate([x[:, :BLK], zero], axis=1),
                                jnp.concatenate([zero, x[:, BLK:]], axis=1)], axis=0)

    def split(x):
        hi = x.astype(BF16)
        return hi, (x - hi.astype(F32)).astype(BF16)

    def product(a, b):
        (a_hi, a_lo), (b_hi, b_lo) = split(a), split(b)
        return dot(jnp.concatenate([a_hi, a_lo, a_hi], axis=1), jnp.concatenate([b_hi, b_hi, b_lo], axis=0))

    def invert(p):
        eye = (lax.broadcasted_iota(jnp.int32, (BLK, BLK), 0)
               == lax.broadcasted_iota(jnp.int32, (BLK, BLK), 1)).astype(F32)
        eye = jnp.concatenate([eye, eye], axis=1)
        upper = jnp.concatenate([mbuf[p, :BLK, :BLK], mbuf[p, BLK:, BLK:]], axis=1)
        parts = split(upper)
        total = eye - upper
        power = dot(parts[0], diagonal(parts[0])).astype(BF16)
        yield
        for step in range(1, 7):
            if step < 6:
                both = dot(jnp.concatenate([total.astype(BF16), power], axis=0), diagonal(power))
                total = total + both[:BLK]
                power = both[BLK:].astype(BF16)
            else:
                total = total + dot(total.astype(BF16), diagonal(power))
            yield
        guess = total.astype(BF16)
        again = dot(jnp.concatenate(parts, axis=0), diagonal(guess))
        yield
        residual = eye - guess.astype(F32) - again[:BLK] - again[BLK:]
        better = guess.astype(F32) + dot(guess, diagonal(residual.astype(BF16)))
        yield
        inner = product(mbuf[p, :BLK, BLK:], better[:, BLK:])
        yield
        corner = -product(better[:, :BLK], inner)
        whole = jnp.concatenate(
            [jnp.concatenate([better[:, :BLK], corner], axis=1),
             jnp.concatenate([jnp.zeros((BLK, BLK), F32), better[:, BLK:]], axis=1)], axis=0)
        hi, lo = split(whole)
        ybuf[p, :wide] = hi
        ybuf[p, wide:2 * wide] = hi
        ybuf[p, 2 * wide:] = lo

    def solved(first, last):
        return jnp.concatenate([ubuf[q] for q in range(first, last)], axis=1)

    def passed(buf, p, first, last):
        return dot(solved(first, last), buf[p, first * wide:last * wide, :])

    def chain(p, known, known_to):
        rhs = vbuf[p * wide:(p + 1) * wide, :].astype(F32).T
        if p > known_to:
            fresh = passed(ebuf, p, known_to, p)
            known = fresh if known is None else known + fresh
        if known is not None:
            rhs = rhs - known * dbuf[p]
        hi, lo = split(rhs)
        ubuf[p] = dot(jnp.concatenate([hi, lo, hi], axis=1), ybuf[p]).astype(BF16)

    def together(steps):
        steps = list(steps)
        while steps:
            steps = [one for one in steps if next(one, True) is None]

    def readout_copy(p, r, half):
        return pltpu.make_async_remote_copy(
            src_ref=obuf.at[p, pl.ds((2 * r + half) * HALF, HALF)], dst_ref=strip(out_ref, me),
            send_sem=o_send.at[2 * p + r, half], recv_sem=o_recv, device_id={"seq": 2 * p + r, "head": half},
            device_id_type=MESH)

    def read(p, known, known_to):
        out = passed(fbuf, p, known_to, p + 1)
        if known is not None:
            out = out + known
        obuf[p] = (out * fden[p]).T.astype(BF16)
        for r in (0, 1):
            for half in (0, 1):
                own = (me == 2 * p + r) & (core == half)

                @pl.when(jnp.logical_not(own))
                def _():
                    readout_copy(p, r, half).start()

                @pl.when(own)
                def _():
                    pltpu.make_async_copy(obuf.at[p, pl.ds((2 * r + half) * HALF, HALF)], strip(out_ref, me),
                                          o_recv).start()

    @pl.when(core == 1)
    def _():
        wait_all(sbuf, st_recv)
        mask(range(pairs - 1))
        wait_rows(kbuf, 0, 0, n // 2)
        keys_over().start()
        wait_rows(wbuf, 1, 0, n // 2)
        for p in range(half_pairs):
            weights(p, True)
        together([invert(p) for p in range(half_pairs)])
        wait_rows(vbuf, 2, 0, n // 2)
        for p in range(half_pairs):
            chain(p, None, 0)
            solved_over(p).start()
        wait_all(kbuf.at[n * HALF:], k_recv)
        wait_rows(qbuf, 3, n // 2, n - 2)
        for p in range(half_pairs, pairs - 1):
            weights(p, False)
        wait_rows(qbuf, 3, 0, n // 2)
        for p in range(half_pairs):
            weights(p, False)
            read(p, None, 0)
        for p in range(half_pairs, pairs - 1):
            known = passed(fbuf, p, 0, p)
            wait_all(ubuf.at[p], u_recv.at[p])
            read(p, known, p)

    @pl.when(core == 0)
    def _():
        last = pairs - 1
        wait_all(sbuf, st_recv)
        mask(range(half_pairs, pairs))
        wait_rows(kbuf, 0, n // 2, n)
        keys_over().start()
        wait_all(kbuf.at[:n * HALF], k_recv)
        wait_rows(wbuf, 1, n // 2, n)
        for p in range(half_pairs, pairs):
            weights(p, True)
        together([invert(p) for p in range(half_pairs, pairs)])
        wait_rows(qbuf, 3, n - 2, n)
        weights(last, False)
        for p in range(half_pairs):
            wait_all(ubuf.at[p], u_recv.at[p])
        known = {p: passed(ebuf, p, 0, half_pairs) for p in range(half_pairs, pairs)}
        known_read = passed(fbuf, last, 0, half_pairs)
        wait_rows(vbuf, 2, n // 2, n)
        for p in range(half_pairs, pairs):
            chain(p, known[p], half_pairs)
            if p < last:
                solved_over(p).start()
        read(last, known_read, half_pairs)

    for stream in range(4):
        @pl.when(core != streams[stream][2])
        def _():
            remote(stream, 0).wait_send()

        def sent(step, carry):
            remote(stream, step).wait_send()
            return carry

        lax.fori_loop(1, n, sent, 0)
    for c in (0, 1):
        @pl.when(core == c)
        def _():
            def starts_sent(step, carry):
                starts_copy(step, c).wait_send()
                return carry

            lax.fori_loop(1, n, starts_sent, 0)

    keys_over().wait_send()

    def sent_by(solves, reads):
        for p in solves:
            solved_over(p).wait_send()
        for p in reads:
            for r in (0, 1):
                for half in (0, 1):
                    @pl.when(jnp.logical_not((me == 2 * p + r) & (core == half)))
                    def _():
                        readout_copy(p, r, half).wait_send()

    @pl.when(core == 1)
    def _():
        sent_by(range(half_pairs), range(pairs - 1))

    @pl.when(core == 0)
    def _():
        sent_by(range(half_pairs, pairs - 1), (pairs - 1,))

    wait_all(out_ref, o_recv)


def solution(mesh):
    n = mesh.shape["seq"]

    def step(queries, keys, writes, values, starts):
        features = queries.shape[1]
        length = n * BLK
        hbm = pl.BlockSpec(memory_space=pl.ANY)
        dma = pltpu.SemaphoreType.DMA
        return pl.pallas_call(
            functools.partial(kernel, n),
            out_shape=jax.ShapeDtypeStruct((HALF, features), BF16),
            in_specs=[hbm] * 5,
            out_specs=hbm,
            scratch_shapes=[
                pltpu.VMEM((length, HD), BF16),
                pltpu.VMEM((length, HD), BF16),
                pltpu.VMEM((length, HD), BF16),
                pltpu.VMEM((length, HD), BF16),
                pltpu.VMEM((n, 1, BLK), jnp.int32),
                pltpu.VMEM((n // 2 * (n // 2 + 1), BLK, 2 * BLK), F32),
                pltpu.VMEM((n // 2, length, 2 * BLK), BF16),
                pltpu.VMEM((n // 2, length, 2 * BLK), BF16),
                pltpu.VMEM((length, 2 * BLK), F32),
                pltpu.VMEM((n // 2, 2 * BLK, 2 * BLK), F32),
                pltpu.VMEM((n // 2, 6 * BLK, 2 * BLK), BF16),
                pltpu.VMEM((n // 2, HD, 2 * BLK), BF16),
                pltpu.VMEM((n // 2, 2 * BLK, HD), BF16),
                pltpu.VMEM((n // 2, 1, 2 * BLK), F32),
                pltpu.VMEM((n // 2, 1, 2 * BLK), F32),
                dma((4, n)),
                dma((n, 2)),
                dma((4, 2)),
                dma,
                dma,
                dma,
                dma((n // 2,)),
                dma((n // 2,)),
                dma((n, 2)),
                dma,
            ],
            compiler_params=pltpu.CompilerParams(collective_id=0, has_side_effects=True,
                                                 vmem_limit_bytes=67_043_328),
        )(queries, keys, writes, values, starts.reshape(1, BLK))

    rows = P(("dp", "seq", "head"), None)
    return jax.shard_map(step, mesh=mesh, in_specs=(rows, rows, rows, rows, P(("dp", "seq"))), out_specs=rows,
                         check_vma=False)
```

```python
import functools
import math

import jax
import jax.numpy as jnp
from jax import lax
from jax.experimental import pallas as pl
from jax.experimental.pallas import tpu as pltpu
from jax.sharding import PartitionSpec as P

HD = 128
BLK = 128
HALF = 64
MASKED = -1e30
SCALE2 = HD ** (-0.5) * math.log2(math.e)
MESH = pl.DeviceIdType.MESH
F32 = jnp.float32
BF16 = jnp.bfloat16
NT = (((1,), (1,)), ((), ()))


def dot(a, b):
    return jnp.dot(a, b, preferred_element_type=F32)


def kernel(n, q_ref, k_ref, w_ref, v_ref, st_ref, out_ref, qbuf, kbuf, wbuf, vbuf, sbuf, bias, ebuf, fbuf, sscr, mbuf,
           ybuf, ubuf, obuf, dbuf, fden, send_sem, st_send, recv_sem, k_send, k_recv, st_recv, u_send, u_recv, o_send,
           o_recv):
    me = lax.axis_index("seq")
    core = lax.axis_index("head")

    def chip(step):
        return lax.rem(me + step, n)

    barrier = pltpu.get_barrier_semaphore()

    def greet(step, carry):
        for c in (0, 1):
            pl.semaphore_signal(barrier, inc=1, device_id={"seq": chip(step), "head": c}, device_id_type=MESH)
        return carry

    lax.fori_loop(1, n, greet, 0)
    pl.semaphore_signal(barrier, inc=1, device_id={"head": 1 - core}, device_id_type=MESH)
    pl.semaphore_wait(barrier, 2 * n - 1)

    my_rows = pl.ds(pl.multiple_of(me * BLK + core * HALF, HALF), HALF)
    half_index = me // (n // 2)
    solver = 1 - half_index
    pairs = n // 2
    late = (6, 7) if pairs == 8 else (pairs - 1,)
    early = tuple(p for p in range(pairs) if p not in late)
    reader = 1
    for p in late:
        reader = jnp.where(me // 2 == p, 0, reader)
    streams = ((k_ref, kbuf, solver), (w_ref, wbuf, solver), (v_ref, vbuf, solver), (q_ref, qbuf, reader))

    def strip(ref, head):
        return ref.at[:, pl.ds(pl.multiple_of(head * HD, HD), HD)]

    def remote(stream, step):
        src, dst, c = streams[stream]
        target = chip(step)
        return pltpu.make_async_remote_copy(
            src_ref=strip(src, target), dst_ref=dst.at[my_rows], send_sem=send_sem.at[stream, step],
            recv_sem=recv_sem.at[stream], device_id={"seq": target, "head": c}, device_id_type=MESH)

    def starts_copy(step, c):
        return pltpu.make_async_remote_copy(
            src_ref=st_ref, dst_ref=sbuf.at[me], send_sem=st_send.at[step, c], recv_sem=st_recv,
            device_id={"seq": chip(step), "head": c}, device_id_type=MESH)

    pltpu.make_async_copy(st_ref, sbuf.at[me], st_recv).start()
    for c in (0, 1):
        @pl.when(core == c)
        def _():
            def send_starts(step, carry):
                starts_copy(step, c).start()
                return carry

            lax.fori_loop(1, n, send_starts, 0)

    def send_stream(stream):
        src, dst, c = streams[stream]

        @pl.when(core == c)
        def _():
            pltpu.make_async_copy(strip(src, me), dst.at[my_rows], recv_sem.at[stream]).start()

        @pl.when(core != c)
        def _():
            remote(stream, 0).start()

        def send(step, carry):
            remote(stream, step).start()
            return carry

        lax.fori_loop(1, n, send, 0)

    for stream in range(4):
        send_stream(stream)

    def wait_all(buf, sem):
        pltpu.make_async_copy(buf, buf, sem).wait()

    def wait_blocks(buf, stream, count):
        wait_all(buf.at[:count * BLK], recv_sem.at[stream])

    def keys_over():
        mine = kbuf.at[pl.ds(pl.multiple_of((1 - core) * (n * HALF), n * HALF), n * HALF)]
        return pltpu.make_async_remote_copy(src_ref=mine, dst_ref=mine, send_sem=k_send, recv_sem=k_recv,
                                            device_id={"head": 1 - core}, device_id_type=MESH)

    def solved_over(p):
        return pltpu.make_async_remote_copy(
            src_ref=ubuf.at[p], dst_ref=ubuf.at[p], send_sem=u_send.at[p], recv_sem=u_recv.at[p],
            device_id={"head": 1 - core}, device_id_type=MESH)

    wide = 2 * BLK

    half_pairs = pairs // 2

    def tile_of(p, j):
        return p * (p + 1) + j

    def mask(which):
        for p in which:
            first = jnp.concatenate([sbuf[2 * p], sbuf[2 * p + 1]], axis=1)
            first = first - lax.broadcasted_iota(jnp.int32, (8, wide), 0)
            for j in range(2 * p + 2):
                key = lax.broadcasted_iota(jnp.int32, (BLK // 8, 8, wide), 0) * 8 + j * BLK
                bias[tile_of(p, j)] = jnp.where(key >= first, 0.0, MASKED).reshape(BLK, wide)

    def weights(p, solve):
        rows = (wbuf if solve else qbuf)[p * wide:(p + 1) * wide, :]
        into, den_into = (ebuf, dbuf) if solve else (fbuf, fden)
        limit = (lax.broadcasted_iota(jnp.int32, (8, wide), 1) + p * wide
                 - lax.broadcasted_iota(jnp.int32, (8, wide), 0))
        top = jnp.full((8, wide), 0.0 if solve else MASKED, F32)
        tiles = 2 * p + 2
        for j in range(tiles):
            score = lax.dot_general(kbuf[j * BLK:(j + 1) * BLK, :], rows, NT, preferred_element_type=F32)
            score = (score + bias[tile_of(p, j)]).reshape(BLK // 8, 8, wide)
            if j >= 2 * p:
                key = lax.broadcasted_iota(jnp.int32, score.shape, 0) * 8 + j * BLK
                score = jnp.where((key < limit) if solve else (key <= limit), score, MASKED)
            top = jnp.maximum(top, jnp.max(score, axis=0))
            sscr[j * BLK:(j + 1) * BLK, :] = score.reshape(BLK, wide)
        peak = jnp.max(top, axis=0, keepdims=True)
        total = jnp.zeros((8, wide), F32)
        for j in range(tiles):
            e = jnp.exp2((sscr[j * BLK:(j + 1) * BLK, :] - peak) * SCALE2)
            total = total + jnp.sum(e.reshape(BLK // 8, 8, wide), axis=0)
            into[p, j * BLK:(j + 1) * BLK, :] = e.astype(BF16)
            if solve and j >= 2 * p:
                mbuf[p, (j - 2 * p) * BLK:(j - 2 * p + 1) * BLK, :] = e
        den = jnp.sum(total, axis=0, keepdims=True)
        if solve:
            den = den + jnp.exp2(-peak * SCALE2)
        den_into[p] = 1.0 / den
        if solve:
            mbuf[p] = mbuf[p] * den_into[p]

    def diagonal(x):
        zero = jnp.zeros((BLK, BLK), BF16)
        return jnp.concatenate([jnp.concatenate([x[:, :BLK], zero], axis=1),
                                jnp.concatenate([zero, x[:, BLK:]], axis=1)], axis=0)

    def split(x):
        hi = x.astype(BF16)
        return hi, (x - hi.astype(F32)).astype(BF16)

    def invert(p):
        eye = (lax.broadcasted_iota(jnp.int32, (BLK, BLK), 0)
               == lax.broadcasted_iota(jnp.int32, (BLK, BLK), 1)).astype(F32)
        eye = jnp.concatenate([eye, eye], axis=1)
        upper = jnp.concatenate([mbuf[p, :BLK, :BLK], mbuf[p, BLK:, BLK:]], axis=1)
        low, rest = split(upper)
        total = eye - upper
        power = dot(low, diagonal(low)).astype(BF16)
        yield
        for step in range(1, 7):
            if step < 6:
                both = dot(jnp.concatenate([total.astype(BF16), power], axis=0), diagonal(power))
                total = total + both[:BLK]
                power = both[BLK:].astype(BF16)
            else:
                total = total + dot(total.astype(BF16), diagonal(power))
            yield
        guess = total.astype(BF16)
        again = dot(jnp.concatenate([low, rest], axis=0), diagonal(guess))
        yield
        residual = eye - guess.astype(F32) - again[:BLK] - again[BLK:]
        better, finer = split(guess.astype(F32) + dot(guess, diagonal(residual.astype(BF16))))
        yield
        inner = dot(mbuf[p, :BLK, BLK:].astype(BF16), better[:, BLK:]).astype(BF16)
        yield
        corner, finer_corner = split(-dot(better[:, :BLK], inner))
        zero = jnp.zeros((BLK, BLK), BF16)
        for k, (x, c) in enumerate(((better, corner), (finer, finer_corner))):
            ybuf[p, k, :BLK, :BLK] = x[:, :BLK]
            ybuf[p, k, :BLK, BLK:] = c
            ybuf[p, k, BLK:, :BLK] = zero
            ybuf[p, k, BLK:, BLK:] = x[:, BLK:]

    def solved(first, last):
        return jnp.concatenate([ubuf[q] for q in range(first, last)], axis=1)

    def passed(buf, p, first, last):
        return dot(solved(first, last), buf[p, first * wide:last * wide, :])

    def chain(p, sums):
        rhs = vbuf[p * wide:(p + 1) * wide, :].astype(F32).T
        if p in sums:
            rhs = rhs - sums[p] * dbuf[p]
        hi, lo = split(rhs)
        ubuf[p] = (dot(hi, ybuf[p, 0]) + dot(hi, ybuf[p, 1]) + lo.astype(F32)).astype(BF16)

    def pass_on(q, which, sums):
        for p in which:
            more = passed(ebuf, p, q, q + 1)
            sums[p] = sums[p] + more if p in sums else more

    def together(steps):
        steps = list(steps)
        while steps:
            steps = [one for one in steps if next(one, True) is None]

    def readout_copy(p, r, half):
        return pltpu.make_async_remote_copy(
            src_ref=obuf.at[p, pl.ds((2 * r + half) * HALF, HALF)], dst_ref=strip(out_ref, me),
            send_sem=o_send.at[2 * p + r, half], recv_sem=o_recv, device_id={"seq": 2 * p + r, "head": half},
            device_id_type=MESH)

    def read(p):
        obuf[p] = (passed(fbuf, p, 0, p + 1) * fden[p]).T.astype(BF16)
        for r in (0, 1):
            for half in (0, 1):
                own = (me == 2 * p + r) & (core == half)

                @pl.when(jnp.logical_not(own))
                def _():
                    readout_copy(p, r, half).start()

                @pl.when(own)
                def _():
                    pltpu.make_async_copy(obuf.at[p, pl.ds((2 * r + half) * HALF, HALF)], strip(out_ref, me),
                                          o_recv).start()

    @pl.when(core == 1)
    def _():
        wait_all(sbuf, st_recv)
        mask(sorted(set(range(half_pairs)) | set(early)))
        wait_blocks(kbuf, 0, n // 2)
        keys_over().start()
        wait_blocks(wbuf, 1, n // 2)
        for p in range(half_pairs):
            weights(p, True)
        together([invert(p) for p in range(half_pairs)])
        wait_blocks(vbuf, 2, n // 2)
        sums = {}
        for p in range(half_pairs):
            chain(p, sums)
            solved_over(p).start()
            pass_on(p, range(p + 1, half_pairs), sums)
        wait_all(kbuf.at[n * HALF:], k_recv)
        wait_blocks(qbuf, 3, 2 * len(early))
        for p in early:
            weights(p, False)
            if p >= half_pairs:
                wait_all(ubuf.at[p], u_recv.at[p])
            read(p)

    @pl.when(core == 0)
    def _():
        wait_all(sbuf, st_recv)
        mask(sorted(set(range(half_pairs, pairs)) | set(late)))
        wait_blocks(kbuf, 0, n // 2)
        keys_over().start()
        wait_all(kbuf.at[:n * HALF], k_recv)
        wait_blocks(wbuf, 1, n // 2)
        for p in range(half_pairs, pairs):
            weights(p, True)
        together([invert(p) for p in range(half_pairs, pairs)])
        wait_blocks(vbuf, 2, n // 2)
        sums = {}
        for q in range(half_pairs):
            wait_all(ubuf.at[q], u_recv.at[q])
            pass_on(q, range(half_pairs, pairs), sums)
        for p in range(half_pairs, pairs):
            chain(p, sums)
            if p in early:
                solved_over(p).start()
            pass_on(p, range(p + 1, pairs), sums)
        wait_blocks(qbuf, 3, 2 * len(late))
        for p in late:
            weights(p, False)
            read(p)

    for stream in range(4):
        @pl.when(core != streams[stream][2])
        def _():
            remote(stream, 0).wait_send()

        def sent(step, carry):
            remote(stream, step).wait_send()
            return carry

        lax.fori_loop(1, n, sent, 0)
    for c in (0, 1):
        @pl.when(core == c)
        def _():
            def starts_sent(step, carry):
                starts_copy(step, c).wait_send()
                return carry

            lax.fori_loop(1, n, starts_sent, 0)

    keys_over().wait_send()

    def sent_by(solves, reads):
        for p in solves:
            solved_over(p).wait_send()
        for p in reads:
            for r in (0, 1):
                for half in (0, 1):
                    @pl.when(jnp.logical_not((me == 2 * p + r) & (core == half)))
                    def _():
                        readout_copy(p, r, half).wait_send()

    @pl.when(core == 1)
    def _():
        sent_by(range(half_pairs), early)

    @pl.when(core == 0)
    def _():
        sent_by([p for p in early if p >= half_pairs], late)

    wait_all(out_ref, o_recv)


def solution(mesh):
    n = mesh.shape["seq"]

    def step(queries, keys, writes, values, starts):
        features = queries.shape[1]
        length = n * BLK
        hbm = pl.BlockSpec(memory_space=pl.ANY)
        dma = pltpu.SemaphoreType.DMA
        return pl.pallas_call(
            functools.partial(kernel, n),
            out_shape=jax.ShapeDtypeStruct((HALF, features), BF16),
            in_specs=[hbm] * 5,
            out_specs=hbm,
            scratch_shapes=[
                pltpu.VMEM((length, HD), BF16),
                pltpu.VMEM((length, HD), BF16),
                pltpu.VMEM((length, HD), BF16),
                pltpu.VMEM((length, HD), BF16),
                pltpu.VMEM((n, 1, BLK), jnp.int32),
                pltpu.VMEM((n // 2 * (n // 2 + 1), BLK, 2 * BLK), F32),
                pltpu.VMEM((n // 2, length, 2 * BLK), BF16),
                pltpu.VMEM((n // 2, length, 2 * BLK), BF16),
                pltpu.VMEM((length, 2 * BLK), F32),
                pltpu.VMEM((n // 2, 2 * BLK, 2 * BLK), F32),
                pltpu.VMEM((n // 2, 2, 2 * BLK, 2 * BLK), BF16),
                pltpu.VMEM((n // 2, HD, 2 * BLK), BF16),
                pltpu.VMEM((n // 2, 2 * BLK, HD), BF16),
                pltpu.VMEM((n // 2, 1, 2 * BLK), F32),
                pltpu.VMEM((n // 2, 1, 2 * BLK), F32),
                dma((4, n)),
                dma((n, 2)),
                dma((4,)),
                dma,
                dma,
                dma,
                dma((n // 2,)),
                dma((n // 2,)),
                dma((n, 2)),
                dma,
            ],
            compiler_params=pltpu.CompilerParams(collective_id=0, has_side_effects=True,
                                                 vmem_limit_bytes=48 * 1024 * 1024),
        )(*(pltpu.with_memory_space_constraint(x, pltpu.HBM)
            for x in (queries, keys, writes, values, starts.reshape(1, BLK))))

    rows = P(("dp", "seq", "head"), None)
    return jax.shard_map(step, mesh=mesh, in_specs=(rows, rows, rows, rows, P(("dp", "seq"))), out_specs=rows,
                         check_vma=False)
```

```python
import functools
import math

import jax
import jax.numpy as jnp
from jax import lax
from jax.experimental import pallas as pl
from jax.experimental.pallas import tpu as pltpu
from jax.sharding import PartitionSpec as P

HD = 128
BLK = 128
HALF = 64
MASKED = -1e30
SCALE2 = HD ** (-0.5) * math.log2(math.e)
MESH = pl.DeviceIdType.MESH
F32 = jnp.float32
BF16 = jnp.bfloat16
NT = (((1,), (1,)), ((), ()))


def dot(a, b):
    return jnp.dot(a, b, preferred_element_type=F32)


def kernel(n, q_ref, k_ref, w_ref, v_ref, st_ref, out_ref, qbuf, kbuf, wbuf, vbuf, sbuf, bias, ebuf, fbuf, sscr, mbuf,
           ybuf, ubuf, obuf, dbuf, fden, send_sem, st_send, recv_sem, k_send, k_recv, st_recv, u_send, u_recv, o_send,
           o_recv):
    me = lax.axis_index("seq")
    core = lax.axis_index("head")

    def chip(step):
        return lax.rem(me + step, n)

    barrier = pltpu.get_barrier_semaphore()

    far = [10, 9, 11, 6, 14, 5, 7, 13, 15, 2, 8, 1, 3, 4, 12]
    for step in [step for step in far if step < n] + list(range(16, n)):
        for c in (0, 1):
            pl.semaphore_signal(barrier, inc=1, device_id={"seq": chip(step), "head": c}, device_id_type=MESH)
    pl.semaphore_signal(barrier, inc=1, device_id={"head": 1 - core}, device_id_type=MESH)
    pl.semaphore_wait(barrier, 2 * n - 1)

    my_rows = pl.ds(pl.multiple_of(me * BLK + core * HALF, HALF), HALF)
    half_index = me // (n // 2)
    solver = 1 - half_index
    pairs = n // 2
    late = (6, 7) if pairs == 8 else (pairs - 1,)
    early = tuple(p for p in range(pairs) if p not in late)
    reader = 1
    for p in late:
        reader = jnp.where(me // 2 == p, 0, reader)
    streams = ((k_ref, kbuf, solver), (w_ref, wbuf, solver), (v_ref, vbuf, solver), (q_ref, qbuf, reader))

    def strip(ref, head):
        return ref.at[:, pl.ds(pl.multiple_of(head * HD, HD), HD)]

    def remote(stream, step):
        src, dst, c = streams[stream]
        target = chip(step)
        return pltpu.make_async_remote_copy(
            src_ref=strip(src, target), dst_ref=dst.at[my_rows], send_sem=send_sem.at[stream, step],
            recv_sem=recv_sem.at[stream], device_id={"seq": target, "head": c}, device_id_type=MESH)

    def starts_copy(step, c):
        return pltpu.make_async_remote_copy(
            src_ref=st_ref, dst_ref=sbuf.at[me], send_sem=st_send.at[step, c], recv_sem=st_recv,
            device_id={"seq": chip(step), "head": c}, device_id_type=MESH)

    rows_on = ([p for p in range(pairs) if p >= pairs // 2 or p in late],
               [p for p in range(pairs) if p < pairs // 2 or p in early])
    wanted = []
    for c in (0, 1):
        found = me < 0
        for p in rows_on[c]:
            found = found | (me // 2 == p)
        wanted.append(found)

    for c in (0, 1):
        @pl.when((core == c) & wanted[c])
        def _():
            pltpu.make_async_copy(st_ref, sbuf.at[me], st_recv).start()

            def send_starts(step, carry):
                starts_copy(step, c).start()
                return carry

            lax.fori_loop(1, n, send_starts, 0)

    def send_stream(stream):
        src, dst, c = streams[stream]

        @pl.when(core == c)
        def _():
            pltpu.make_async_copy(strip(src, me), dst.at[my_rows], recv_sem.at[stream]).start()

        @pl.when(core != c)
        def _():
            remote(stream, 0).start()

        def send(step, carry):
            remote(stream, step).start()
            return carry

        lax.fori_loop(1, n, send, 0)

    for stream in range(4):
        send_stream(stream)

    def wait_all(buf, sem):
        pltpu.make_async_copy(buf, buf, sem).wait()

    def wait_blocks(buf, stream, count):
        wait_all(buf.at[:count * BLK], recv_sem.at[stream])

    def keys_over():
        mine = kbuf.at[pl.ds(pl.multiple_of((1 - core) * (n * HALF), n * HALF), n * HALF)]
        return pltpu.make_async_remote_copy(src_ref=mine, dst_ref=mine, send_sem=k_send, recv_sem=k_recv,
                                            device_id={"head": 1 - core}, device_id_type=MESH)

    def solved_over(p):
        return pltpu.make_async_remote_copy(
            src_ref=ubuf.at[p], dst_ref=ubuf.at[p], send_sem=u_send.at[p], recv_sem=u_recv.at[p],
            device_id={"head": 1 - core}, device_id_type=MESH)

    wide = 2 * BLK

    half_pairs = pairs // 2

    def tile_of(p, j):
        return p * (p + 1) + j

    def mask(which):
        for p in which:
            first = jnp.concatenate([sbuf[2 * p], sbuf[2 * p + 1]], axis=1)
            first = first - lax.broadcasted_iota(jnp.int32, (8, wide), 0)
            for j in range(2 * p + 2):
                key = lax.broadcasted_iota(jnp.int32, (BLK // 8, 8, wide), 0) * 8 + j * BLK
                bias[tile_of(p, j)] = jnp.where(key >= first, 0.0, MASKED).reshape(BLK, wide)

    def weights(p, solve):
        rows = (wbuf if solve else qbuf)[p * wide:(p + 1) * wide, :]
        into, den_into = (ebuf, dbuf) if solve else (fbuf, fden)
        limit = (lax.broadcasted_iota(jnp.int32, (8, wide), 1) + p * wide
                 - lax.broadcasted_iota(jnp.int32, (8, wide), 0))
        top = jnp.full((8, wide), 0.0 if solve else MASKED, F32)
        tiles = 2 * p + 2
        for j in range(tiles):
            score = lax.dot_general(kbuf[j * BLK:(j + 1) * BLK, :], rows, NT, preferred_element_type=F32)
            score = (score + bias[tile_of(p, j)]).reshape(BLK // 8, 8, wide)
            if j >= 2 * p:
                key = lax.broadcasted_iota(jnp.int32, score.shape, 0) * 8 + j * BLK
                score = jnp.where((key < limit) if solve else (key <= limit), score, MASKED)
            top = jnp.maximum(top, jnp.max(score, axis=0))
            sscr[j * BLK:(j + 1) * BLK, :] = score.reshape(BLK, wide)
        peak = jnp.max(top, axis=0, keepdims=True)
        total = jnp.zeros((8, wide), F32)
        for j in range(tiles):
            e = jnp.exp2((sscr[j * BLK:(j + 1) * BLK, :] - peak) * SCALE2)
            total = total + jnp.sum(e.reshape(BLK // 8, 8, wide), axis=0)
            into[p, j * BLK:(j + 1) * BLK, :] = e.astype(BF16)
            if solve and j >= 2 * p:
                mbuf[p, (j - 2 * p) * BLK:(j - 2 * p + 1) * BLK, :] = e
        den = jnp.sum(total, axis=0, keepdims=True)
        if solve:
            den = den + jnp.exp2(-peak * SCALE2)
        den_into[p] = 1.0 / den
        if solve:
            mbuf[p] = mbuf[p] * den_into[p]

    def diagonal(x):
        zero = jnp.zeros((BLK, BLK), BF16)
        return jnp.concatenate([jnp.concatenate([x[:, :BLK], zero], axis=1),
                                jnp.concatenate([zero, x[:, BLK:]], axis=1)], axis=0)

    def split(x):
        hi = x.astype(BF16)
        return hi, (x - hi.astype(F32)).astype(BF16)

    def invert(p):
        eye = (lax.broadcasted_iota(jnp.int32, (BLK, BLK), 0)
               == lax.broadcasted_iota(jnp.int32, (BLK, BLK), 1)).astype(F32)
        eye = jnp.concatenate([eye, eye], axis=1)
        upper = jnp.concatenate([mbuf[p, :BLK, :BLK], mbuf[p, BLK:, BLK:]], axis=1)
        low, rest = split(upper)
        total = eye - upper
        power = dot(low, diagonal(low)).astype(BF16)
        yield
        for step in range(1, 7):
            if step < 6:
                both = dot(jnp.concatenate([total.astype(BF16), power], axis=0), diagonal(power))
                total = total + both[:BLK]
                power = both[BLK:].astype(BF16)
            else:
                total = total + dot(total.astype(BF16), diagonal(power))
            yield
        guess = total.astype(BF16)
        again = dot(jnp.concatenate([low, rest], axis=0), diagonal(guess))
        yield
        residual = eye - guess.astype(F32) - again[:BLK] - again[BLK:]
        better, finer = split(guess.astype(F32) + dot(guess, diagonal(residual.astype(BF16))))
        yield
        inner = dot(mbuf[p, :BLK, BLK:].astype(BF16), better[:, BLK:]).astype(BF16)
        yield
        corner, finer_corner = split(-dot(better[:, :BLK], inner))
        zero = jnp.zeros((BLK, BLK), BF16)
        for k, (x, c) in enumerate(((better, corner), (finer, finer_corner))):
            ybuf[p, k, :BLK, :BLK] = x[:, :BLK]
            ybuf[p, k, :BLK, BLK:] = c
            ybuf[p, k, BLK:, :BLK] = zero
            ybuf[p, k, BLK:, BLK:] = x[:, BLK:]

    def solved(first, last):
        return jnp.concatenate([ubuf[q] for q in range(first, last)], axis=1)

    def passed(buf, p, first, last):
        return dot(solved(first, last), buf[p, first * wide:last * wide, :])

    def chain(p, sums):
        rhs = vbuf[p * wide:(p + 1) * wide, :].astype(F32).T
        if p in sums:
            rhs = rhs - sums[p] * dbuf[p]
        hi, lo = split(rhs)
        ubuf[p] = (dot(hi, ybuf[p, 0]) + dot(hi, ybuf[p, 1]) + lo.astype(F32)).astype(BF16)

    def pass_on(q, which, sums):
        for p in which:
            more = passed(ebuf, p, q, q + 1)
            sums[p] = sums[p] + more if p in sums else more

    def together(steps):
        steps = list(steps)
        while steps:
            steps = [one for one in steps if next(one, True) is None]

    def readout_copy(p, r, half):
        return pltpu.make_async_remote_copy(
            src_ref=obuf.at[p, pl.ds((2 * r + half) * HALF, HALF)], dst_ref=strip(out_ref, me),
            send_sem=o_send.at[2 * p + r, half], recv_sem=o_recv, device_id={"seq": 2 * p + r, "head": half},
            device_id_type=MESH)

    def read(p):
        obuf[p] = (passed(fbuf, p, 0, p + 1) * fden[p]).T.astype(BF16)

    def hand_out(p):
        for r in (0, 1):
            for half in (0, 1):
                own = (me == 2 * p + r) & (core == half)

                @pl.when(jnp.logical_not(own))
                def _():
                    readout_copy(p, r, half).start()

                @pl.when(own)
                def _():
                    pltpu.make_async_copy(obuf.at[p, pl.ds((2 * r + half) * HALF, HALF)], strip(out_ref, me),
                                          o_recv).start()

    def read_out(which, awaited):
        for p in which:
            weights(p, False)
        for p in awaited:
            wait_all(ubuf.at[p], u_recv.at[p])
        for p in which:
            read(p)
        for p in which:
            hand_out(p)

    @pl.when(core == 1)
    def _():
        wait_all(sbuf.at[:2 * len(rows_on[1])], st_recv)
        mask(sorted(set(range(half_pairs)) | set(early)))
        wait_blocks(kbuf, 0, n // 2)
        keys_over().start()
        wait_blocks(wbuf, 1, n // 2)
        for p in range(half_pairs):
            weights(p, True)
        together([invert(p) for p in range(half_pairs)])
        wait_blocks(vbuf, 2, n // 2)
        sums = {}
        for p in range(half_pairs):
            chain(p, sums)
            solved_over(p).start()
            pass_on(p, range(p + 1, half_pairs), sums)
        wait_all(kbuf.at[n * HALF:], k_recv)
        wait_blocks(qbuf, 3, 2 * len(early))
        for k in range(0, len(early), 2):
            read_out(early[k:k + 2], [p for p in early[k:k + 2] if p >= half_pairs])

    @pl.when(core == 0)
    def _():
        wait_all(sbuf.at[:2 * len(rows_on[0])], st_recv)
        mask(sorted(set(range(half_pairs, pairs)) | set(late)))
        wait_blocks(kbuf, 0, n // 2)
        keys_over().start()
        wait_all(kbuf.at[:n * HALF], k_recv)
        wait_blocks(wbuf, 1, n // 2)
        for p in range(half_pairs, pairs):
            weights(p, True)
        together([invert(p) for p in range(half_pairs, pairs)])
        wait_blocks(vbuf, 2, n // 2)
        sums = {}
        for q in range(half_pairs):
            wait_all(ubuf.at[q], u_recv.at[q])
            pass_on(q, range(half_pairs, pairs), sums)
        for p in range(half_pairs, pairs):
            chain(p, sums)
            if p in early:
                solved_over(p).start()
            pass_on(p, range(p + 1, pairs), sums)
        wait_blocks(qbuf, 3, 2 * len(late))
        for p in late:
            read_out((p,), ())

    for stream in range(4):
        @pl.when(core != streams[stream][2])
        def _():
            remote(stream, 0).wait_send()

        def sent(step, carry):
            remote(stream, step).wait_send()
            return carry

        lax.fori_loop(1, n, sent, 0)
    for c in (0, 1):
        @pl.when((core == c) & wanted[c])
        def _():
            def starts_sent(step, carry):
                starts_copy(step, c).wait_send()
                return carry

            lax.fori_loop(1, n, starts_sent, 0)

    keys_over().wait_send()

    def sent_by(solves, reads):
        for p in solves:
            solved_over(p).wait_send()
        for p in reads:
            for r in (0, 1):
                for half in (0, 1):
                    @pl.when(jnp.logical_not((me == 2 * p + r) & (core == half)))
                    def _():
                        readout_copy(p, r, half).wait_send()

    @pl.when(core == 1)
    def _():
        sent_by(range(half_pairs), early)

    @pl.when(core == 0)
    def _():
        sent_by([p for p in early if p >= half_pairs], late)

    wait_all(out_ref, o_recv)


def solution(mesh):
    n = mesh.shape["seq"]

    def step(queries, keys, writes, values, starts):
        features = queries.shape[1]
        length = n * BLK
        hbm = pl.BlockSpec(memory_space=pl.ANY)
        dma = pltpu.SemaphoreType.DMA
        return pl.pallas_call(
            functools.partial(kernel, n),
            out_shape=jax.ShapeDtypeStruct((HALF, features), BF16),
            in_specs=[hbm] * 5,
            out_specs=hbm,
            scratch_shapes=[
                pltpu.VMEM((length, HD), BF16),
                pltpu.VMEM((length, HD), BF16),
                pltpu.VMEM((length, HD), BF16),
                pltpu.VMEM((length, HD), BF16),
                pltpu.VMEM((n, 1, BLK), jnp.int32),
                pltpu.VMEM((n // 2 * (n // 2 + 1), BLK, 2 * BLK), F32),
                pltpu.VMEM((n // 2, length, 2 * BLK), BF16),
                pltpu.VMEM((n // 2, length, 2 * BLK), BF16),
                pltpu.VMEM((length, 2 * BLK), F32),
                pltpu.VMEM((n // 2, 2 * BLK, 2 * BLK), F32),
                pltpu.VMEM((n // 2, 2, 2 * BLK, 2 * BLK), BF16),
                pltpu.VMEM((n // 2, HD, 2 * BLK), BF16),
                pltpu.VMEM((n // 2, 2 * BLK, HD), BF16),
                pltpu.VMEM((n // 2, 1, 2 * BLK), F32),
                pltpu.VMEM((n // 2, 1, 2 * BLK), F32),
                dma((4, n)),
                dma((n, 2)),
                dma((4,)),
                dma,
                dma,
                dma,
                dma((n // 2,)),
                dma((n // 2,)),
                dma((n, 2)),
                dma,
            ],
            compiler_params=pltpu.CompilerParams(collective_id=0, has_side_effects=True,
                                                 vmem_limit_bytes=48 * 1024 * 1024),
        )(*(pltpu.with_memory_space_constraint(x, pltpu.HBM)
            for x in (queries, keys, writes, values, starts.reshape(1, BLK))))

    rows = P(("dp", "seq", "head"), None)
    return jax.shard_map(step, mesh=mesh, in_specs=(rows, rows, rows, rows, P(("dp", "seq"))), out_specs=rows,
                         check_vma=False)
```

```python
import functools
import math

import jax
import jax.numpy as jnp
from jax import lax
from jax.experimental import pallas as pl
from jax.experimental.pallas import tpu as pltpu
from jax.sharding import PartitionSpec as P

HD = 128
BLK = 128
HALF = 64
MASKED = -1e30
SCALE2 = HD ** (-0.5) * math.log2(math.e)
MESH = pl.DeviceIdType.MESH
F32 = jnp.float32
BF16 = jnp.bfloat16
NT = (((1,), (1,)), ((), ()))


def dot(a, b):
    return jnp.dot(a, b, preferred_element_type=F32)


def kernel(n, q_ref, k_ref, w_ref, v_ref, st_ref, out_ref, qbuf, kbuf, wbuf, vbuf, sbuf, bias, ebuf, fbuf, sscr, mbuf,
           ybuf, ubuf, obuf, dbuf, fden, send_sem, st_send, recv_sem, k_send, k_recv, st_recv, u_send, u_recv, o_send,
           o_recv):
    me = lax.axis_index("seq")
    core = lax.axis_index("head")

    def chip(step):
        return lax.rem(me + step, n)

    barrier = pltpu.get_barrier_semaphore()

    far = [10, 9, 11, 6, 14, 5, 7, 13, 15, 2, 8, 1, 3, 4, 12]
    for step in [step for step in far if step < n] + list(range(16, n)):
        for c in (0, 1):
            pl.semaphore_signal(barrier, inc=1, device_id={"seq": chip(step), "head": c}, device_id_type=MESH)
    pl.semaphore_signal(barrier, inc=1, device_id={"head": 1 - core}, device_id_type=MESH)
    pl.semaphore_wait(barrier, 2 * n - 1)

    my_rows = pl.ds(pl.multiple_of(me * BLK + core * HALF, HALF), HALF)
    half_index = me // (n // 2)
    solver = 1 - half_index
    pairs = n // 2
    late = (6, 7) if pairs == 8 else (pairs - 1,)
    early = tuple(p for p in range(pairs) if p not in late)
    reader = 1
    for p in late:
        reader = jnp.where(me // 2 == p, 0, reader)
    streams = ((k_ref, kbuf, solver), (w_ref, wbuf, solver), (v_ref, vbuf, solver), (q_ref, qbuf, reader))

    def strip(ref, head):
        return ref.at[:, pl.ds(pl.multiple_of(head * HD, HD), HD)]

    def remote(stream, step):
        src, dst, c = streams[stream]
        target = chip(step)
        return pltpu.make_async_remote_copy(
            src_ref=strip(src, target), dst_ref=dst.at[my_rows], send_sem=send_sem.at[stream, step],
            recv_sem=recv_sem.at[stream], device_id={"seq": target, "head": c}, device_id_type=MESH)

    def starts_copy(step, c):
        return pltpu.make_async_remote_copy(
            src_ref=st_ref, dst_ref=sbuf.at[me], send_sem=st_send.at[step, c], recv_sem=st_recv,
            device_id={"seq": chip(step), "head": c}, device_id_type=MESH)

    rows_on = ([p for p in range(pairs) if p >= pairs // 2 or p in late],
               [p for p in range(pairs) if p < pairs // 2 or p in early])
    wanted = []
    for c in (0, 1):
        found = me < 0
        for p in rows_on[c]:
            found = found | (me // 2 == p)
        wanted.append(found)

    for c in (0, 1):
        @pl.when((core == c) & wanted[c])
        def _():
            pltpu.make_async_copy(st_ref, sbuf.at[me], st_recv).start()

            def send_starts(step, carry):
                starts_copy(step, c).start()
                return carry

            lax.fori_loop(1, n, send_starts, 0)

    def send_stream(stream):
        src, dst, c = streams[stream]

        @pl.when(core == c)
        def _():
            pltpu.make_async_copy(strip(src, me), dst.at[my_rows], recv_sem.at[stream]).start()

        @pl.when(core != c)
        def _():
            remote(stream, 0).start()

        def send(step, carry):
            remote(stream, step).start()
            return carry

        lax.fori_loop(1, n, send, 0)

    for stream in range(4):
        send_stream(stream)

    def wait_all(buf, sem):
        pltpu.make_async_copy(buf, buf, sem).wait()

    def wait_blocks(buf, stream, count):
        wait_all(buf.at[:count * BLK], recv_sem.at[stream])

    def keys_over():
        mine = kbuf.at[pl.ds(pl.multiple_of((1 - core) * (n * HALF), n * HALF), n * HALF)]
        return pltpu.make_async_remote_copy(src_ref=mine, dst_ref=mine, send_sem=k_send, recv_sem=k_recv,
                                            device_id={"head": 1 - core}, device_id_type=MESH)

    def solved_over(p):
        return pltpu.make_async_remote_copy(
            src_ref=ubuf.at[p], dst_ref=ubuf.at[p], send_sem=u_send.at[p], recv_sem=u_recv.at[p],
            device_id={"head": 1 - core}, device_id_type=MESH)

    wide = 2 * BLK

    half_pairs = pairs // 2

    def tile_of(p, j):
        return p * (p + 1) + j

    def mask(which):
        for p in which:
            first = jnp.concatenate([sbuf[2 * p], sbuf[2 * p + 1]], axis=1)
            first = first - lax.broadcasted_iota(jnp.int32, (8, wide), 0)
            for j in range(2 * p + 2):
                key = lax.broadcasted_iota(jnp.int32, (BLK // 8, 8, wide), 0) * 8 + j * BLK
                bias[tile_of(p, j)] = jnp.where(key >= first, 0.0, MASKED).reshape(BLK, wide)

    def weights(p, solve):
        rows = (wbuf if solve else qbuf)[p * wide:(p + 1) * wide, :]
        into, den_into = (ebuf, dbuf) if solve else (fbuf, fden)
        limit = (lax.broadcasted_iota(jnp.int32, (8, wide), 1) + p * wide
                 - lax.broadcasted_iota(jnp.int32, (8, wide), 0))
        top = jnp.full((8, wide), 0.0 if solve else MASKED, F32)
        tiles = 2 * p + 2
        for j in range(tiles):
            score = lax.dot_general(kbuf[j * BLK:(j + 1) * BLK, :], rows, NT, preferred_element_type=F32)
            score = (score + bias[tile_of(p, j)]).reshape(BLK // 8, 8, wide)
            if j >= 2 * p:
                key = lax.broadcasted_iota(jnp.int32, score.shape, 0) * 8 + j * BLK
                score = jnp.where((key < limit) if solve else (key <= limit), score, MASKED)
            top = jnp.maximum(top, jnp.max(score, axis=0))
            sscr[j * BLK:(j + 1) * BLK, :] = score.reshape(BLK, wide)
        peak = jnp.max(top, axis=0, keepdims=True)
        total = jnp.zeros((8, wide), F32)
        for j in range(tiles):
            e = jnp.exp2((sscr[j * BLK:(j + 1) * BLK, :] - peak) * SCALE2)
            total = total + jnp.sum(e.reshape(BLK // 8, 8, wide), axis=0)
            into[p, j * BLK:(j + 1) * BLK, :] = e.astype(BF16)
            if solve and j >= 2 * p:
                mbuf[p, (j - 2 * p) * BLK:(j - 2 * p + 1) * BLK, :] = e
        den = jnp.sum(total, axis=0, keepdims=True)
        if solve:
            den = den + jnp.exp2(-peak * SCALE2)
        den_into[p] = 1.0 / den
        if solve:
            mbuf[p] = mbuf[p] * den_into[p]

    def diagonal(x):
        zero = jnp.zeros((BLK, BLK), BF16)
        return jnp.concatenate([jnp.concatenate([x[:, :BLK], zero], axis=1),
                                jnp.concatenate([zero, x[:, BLK:]], axis=1)], axis=0)

    def split(x):
        hi = x.astype(BF16)
        return hi, (x - hi.astype(F32)).astype(BF16)

    def invert(p):
        eye = (lax.broadcasted_iota(jnp.int32, (BLK, BLK), 0)
               == lax.broadcasted_iota(jnp.int32, (BLK, BLK), 1)).astype(F32)
        eye = jnp.concatenate([eye, eye], axis=1)
        upper = jnp.concatenate([mbuf[p, :BLK, :BLK], mbuf[p, BLK:, BLK:]], axis=1)
        low, rest = split(upper)
        total = eye - upper
        power = dot(low, diagonal(low)).astype(BF16)
        yield
        for step in range(1, 7):
            if step < 6:
                both = dot(jnp.concatenate([total.astype(BF16), power], axis=0), diagonal(power))
                total = total + both[:BLK]
                power = both[BLK:].astype(BF16)
            else:
                total = total + dot(total.astype(BF16), diagonal(power))
            yield
        guess = total.astype(BF16)
        again = dot(jnp.concatenate([low, rest], axis=0), diagonal(guess))
        yield
        residual = eye - guess.astype(F32) - again[:BLK] - again[BLK:]
        better, finer = split(guess.astype(F32) + dot(guess, diagonal(residual.astype(BF16))))
        yield
        inner = dot(mbuf[p, :BLK, BLK:].astype(BF16), better[:, BLK:]).astype(BF16)
        yield
        corner, finer_corner = split(-dot(better[:, :BLK], inner))
        zero = jnp.zeros((BLK, BLK), BF16)
        for k, (x, c) in enumerate(((better, corner), (finer, finer_corner))):
            ybuf[p, k, :BLK, :BLK] = x[:, :BLK]
            ybuf[p, k, :BLK, BLK:] = c
            ybuf[p, k, BLK:, :BLK] = zero
            ybuf[p, k, BLK:, BLK:] = x[:, BLK:]

    def solved(first, last):
        return jnp.concatenate([ubuf[q] for q in range(first, last)], axis=1)

    def passed(buf, p, first, last):
        return dot(solved(first, last), buf[p, first * wide:last * wide, :])

    def chain(p, sums):
        rhs = vbuf[p * wide:(p + 1) * wide, :].T.astype(F32)
        if p in sums:
            rhs = rhs - sums[p] * dbuf[p]
        hi, lo = split(rhs)
        ubuf[p] = (dot(hi, ybuf[p, 0]) + dot(hi, ybuf[p, 1]) + lo.astype(F32)).astype(BF16)

    def pass_on(q, which, sums):
        for p in which:
            more = passed(ebuf, p, q, q + 1)
            sums[p] = sums[p] + more if p in sums else more

    def together(steps):
        steps = list(steps)
        while steps:
            steps = [one for one in steps if next(one, True) is None]

    def readout_copy(p, r, half):
        return pltpu.make_async_remote_copy(
            src_ref=obuf.at[p, pl.ds((2 * r + half) * HALF, HALF)], dst_ref=strip(out_ref, me),
            send_sem=o_send.at[2 * p + r, half], recv_sem=o_recv, device_id={"seq": 2 * p + r, "head": half},
            device_id_type=MESH)

    def read(p):
        obuf[p] = (passed(fbuf, p, 0, p + 1) * fden[p]).astype(BF16).T

    def hand_out(p):
        for r in (0, 1):
            for half in (0, 1):
                own = (me == 2 * p + r) & (core == half)

                @pl.when(jnp.logical_not(own))
                def _():
                    readout_copy(p, r, half).start()

                @pl.when(own)
                def _():
                    pltpu.make_async_copy(obuf.at[p, pl.ds((2 * r + half) * HALF, HALF)], strip(out_ref, me),
                                          o_recv).start()

    def read_out(which, awaited):
        for p in which:
            weights(p, False)
        for p in awaited:
            wait_all(ubuf.at[p], u_recv.at[p])
        for p in which:
            read(p)
        for p in which:
            hand_out(p)

    @pl.when(core == 1)
    def _():
        wait_all(sbuf.at[:2 * len(rows_on[1])], st_recv)
        mask(sorted(set(range(half_pairs)) | set(early)))
        wait_blocks(kbuf, 0, n // 2)
        keys_over().start()
        wait_blocks(wbuf, 1, n // 2)
        for p in range(half_pairs):
            weights(p, True)
        together([invert(p) for p in range(half_pairs)])
        wait_blocks(vbuf, 2, n // 2)
        sums = {}
        for p in range(half_pairs):
            chain(p, sums)
            solved_over(p).start()
            pass_on(p, range(p + 1, half_pairs), sums)
        wait_all(kbuf.at[n * HALF:], k_recv)
        wait_blocks(qbuf, 3, 2 * len(early))
        for k in range(0, len(early), 2):
            read_out(early[k:k + 2], [p for p in early[k:k + 2] if p >= half_pairs])

    @pl.when(core == 0)
    def _():
        wait_all(sbuf.at[:2 * len(rows_on[0])], st_recv)
        mask(sorted(set(range(half_pairs, pairs)) | set(late)))
        wait_blocks(kbuf, 0, n // 2)
        keys_over().start()
        wait_all(kbuf.at[:n * HALF], k_recv)
        wait_blocks(wbuf, 1, n // 2)
        for p in range(half_pairs, pairs):
            weights(p, True)
        together([invert(p) for p in range(half_pairs, pairs)])
        wait_blocks(vbuf, 2, n // 2)
        sums = {}
        for q in range(half_pairs):
            wait_all(ubuf.at[q], u_recv.at[q])
            pass_on(q, range(half_pairs, pairs), sums)
        for p in range(half_pairs, pairs):
            chain(p, sums)
            if p in early:
                solved_over(p).start()
            pass_on(p, range(p + 1, pairs), sums)
        wait_blocks(qbuf, 3, 2 * len(late))
        for p in late:
            read_out((p,), ())

    for stream in range(4):
        @pl.when(core != streams[stream][2])
        def _():
            remote(stream, 0).wait_send()

        def sent(step, carry):
            remote(stream, step).wait_send()
            return carry

        lax.fori_loop(1, n, sent, 0)
    for c in (0, 1):
        @pl.when((core == c) & wanted[c])
        def _():
            def starts_sent(step, carry):
                starts_copy(step, c).wait_send()
                return carry

            lax.fori_loop(1, n, starts_sent, 0)

    keys_over().wait_send()

    def sent_by(solves, reads):
        for p in solves:
            solved_over(p).wait_send()
        for p in reads:
            for r in (0, 1):
                for half in (0, 1):
                    @pl.when(jnp.logical_not((me == 2 * p + r) & (core == half)))
                    def _():
                        readout_copy(p, r, half).wait_send()

    @pl.when(core == 1)
    def _():
        sent_by(range(half_pairs), early)

    @pl.when(core == 0)
    def _():
        sent_by([p for p in early if p >= half_pairs], late)

    wait_all(out_ref, o_recv)


def solution(mesh):
    n = mesh.shape["seq"]

    def step(queries, keys, writes, values, starts):
        features = queries.shape[1]
        length = n * BLK
        hbm = pl.BlockSpec(memory_space=pl.ANY)
        dma = pltpu.SemaphoreType.DMA
        return pl.pallas_call(
            functools.partial(kernel, n),
            out_shape=jax.ShapeDtypeStruct((HALF, features), BF16),
            in_specs=[hbm] * 5,
            out_specs=hbm,
            scratch_shapes=[
                pltpu.VMEM((length, HD), BF16),
                pltpu.VMEM((length, HD), BF16),
                pltpu.VMEM((length, HD), BF16),
                pltpu.VMEM((length, HD), BF16),
                pltpu.VMEM((n, 1, BLK), jnp.int32),
                pltpu.VMEM((n // 2 * (n // 2 + 1), BLK, 2 * BLK), F32),
                pltpu.VMEM((n // 2, length, 2 * BLK), BF16),
                pltpu.VMEM((n // 2, length, 2 * BLK), BF16),
                pltpu.VMEM((length, 2 * BLK), F32),
                pltpu.VMEM((n // 2, 2 * BLK, 2 * BLK), F32),
                pltpu.VMEM((n // 2, 2, 2 * BLK, 2 * BLK), BF16),
                pltpu.VMEM((n // 2, HD, 2 * BLK), BF16),
                pltpu.VMEM((n // 2, 2 * BLK, HD), BF16),
                pltpu.VMEM((n // 2, 1, 2 * BLK), F32),
                pltpu.VMEM((n // 2, 1, 2 * BLK), F32),
                dma((4, n)),
                dma((n, 2)),
                dma((4,)),
                dma,
                dma,
                dma,
                dma((n // 2,)),
                dma((n // 2,)),
                dma((n, 2)),
                dma,
            ],
            compiler_params=pltpu.CompilerParams(collective_id=0, has_side_effects=True,
                                                 vmem_limit_bytes=48 * 1024 * 1024),
        )(*(pltpu.with_memory_space_constraint(x, pltpu.HBM)
            for x in (queries, keys, writes, values, starts.reshape(1, BLK))))

    rows = P(("dp", "seq", "head"), None)
    return jax.shard_map(step, mesh=mesh, in_specs=(rows, rows, rows, rows, P(("dp", "seq"))), out_specs=rows,
                         check_vma=False)
```
